32 devices in a mesh: shard: 8 (over z, y), ctx: 2 (over x), tensor: 2 (over core).
Axes of the slice: x: 2, y: 2, z: 4, core: 2. Of those that a mesh axis runs over, the one named last changes fastest.
Arguments:
- tokens: bfloat16 [8, 768, 1024], P('shard', 'ctx'), may hold values from -6 to 6
- condition: bfloat16 [8, 1024], P('shard'), may hold values from -6 to 6
- ada_weight: bfloat16 [1024, 6, 1024], P('shard', None, 'tensor'), may hold values from -0.1875 to 0.1875
- ada_bias: float32 [6, 1024], P(None, 'tensor'), may hold values from -4 to 4
- qkv_weight: bfloat16 [1024, 3, 1024], P('shard', None, 'tensor'), may hold values from -0.1875 to 0.1875
- qv_bias: float32 [2, 1024], P(None, 'tensor'), may hold values from -4 to 4
- output_weight: bfloat16 [1024, 1024], P('tensor', 'shard'), may hold values from -3 to 3
- output_bias: float32 [1024], replicated, may hold values from -6 to 6
- expand_weight: bfloat16 [1024, 4096], P('shard', 'tensor'), may hold values from -0.1875 to 0.1875
- expand_bias: float32 [4096], P('tensor'), may hold values from -6 to 6
- contract_weight: bfloat16 [4096, 1024], P('tensor', 'shard'), may hold values from -0.375 to 0.375
- contract_bias: float32 [1024], replicated, may hold values from -6 to 6
- cotangent: bfloat16 [8, 768, 1024], P('shard', 'ctx'), may hold values from -6 to 6
Outputs:
- block_out: float32 [8, 768, 1024], P('shard', 'ctx')
- grad_tokens: float32 [8, 768, 1024], P('shard', 'ctx')
- grad_condition: float32 [8, 1024], P('shard')
- grad_ada_weight: float32 [1024, 6, 1024], P(('shard', 'ctx'), None, 'tensor')
- grad_ada_bias: float32 [6, 1024], P(None, 'tensor')
- grad_qkv_weight: float32 [1024, 3, 1024], P(('shard', 'ctx'), None, 'tensor')
- grad_qv_bias: float32 [2, 1024], P(None, 'tensor')
- grad_output_weight: float32 [1024, 1024], P('tensor', ('shard', 'ctx'))
- grad_output_bias: float32 [1024], replicated
- grad_expand_weight: float32 [1024, 4096], P(('shard', 'ctx'), 'tensor')
- grad_expand_bias: float32 [4096], P('tensor')
- grad_contract_weight: float32 [4096, 1024], P('tensor', ('shard', 'ctx'))
- grad_contract_bias: float32 [1024], replicated
The draws below stay inside these ranges and needn't reach their ends.
All inputs are finite; a program needn't handle non-finite values.
Results may differ from the reference program's by a relative error of at most 0.0117.
The reference program's roundings to bfloat16 on the way count: a program that leaves them out, or rounds other values in their place, can miss the bound.
Values may be sent and summed in bfloat16 or wider, within the bound.
No kernel may reach another device: no remote copies, remote signals or barrier semaphores. Data moves between devices by JAX's collectives and lax.ppermute only.
A program may use at most 128 MiB of HBM per device.

```python
import jax
import jax.numpy as jnp
from jax import lax

D = 1024
HEADS = 16
HD = 64
FF = 4096
SEQ = 768
LATENTS = 8


def block_levels(rng, dims, pieces, smallest, largest):
    gain, own = 1.0, jax.random.fold_in(rng, 6)
    for position, parts in pieces:
        steps = jnp.exp(jax.random.uniform(jax.random.fold_in(own, position), (parts,), jnp.float32, smallest / len(pieces), largest / len(pieces)))
        gain = gain * jnp.repeat(steps, dims[position] // parts).reshape([-1 if axis == position else 1 for axis in range(len(dims))])
    return gain


def noise(key, extent, width, bound, split=(), kind=jnp.bfloat16):
    values = width * jax.random.normal(key, extent, jnp.float32)
    if split:
        values = values * block_levels(key, extent, split, -0.22, 0.18)
    return jnp.clip(values, -bound, bound).astype(kind)


def setup_inputs(seed: int = 0) -> dict:
    arg_keys = jax.random.split(jax.random.key(seed), 14)
    return {
        "tokens": noise(arg_keys[0], (LATENTS, SEQ, D), 1.0, 6.0, ((0, 8), (1, 2))),
        "condition": noise(arg_keys[1], (LATENTS, D), 1.0, 6.0, ((0, 8),)),
        "ada_weight": noise(arg_keys[2], (D, 6, D), D ** -0.5, 0.1875, ((0, 8), (2, 2))),
        "ada_bias": noise(arg_keys[3], (6, D), 0.3, 4.0, ((1, 2),), jnp.float32),
        "qkv_weight": noise(arg_keys[4], (D, 3, D), D ** -0.5, 0.1875, ((0, 8), (2, 2))),
        "qv_bias": noise(arg_keys[5], (2, D), 0.3, 4.0, ((1, 2),), jnp.float32),
        "output_weight": noise(arg_keys[6], (D, D), (max(1, D // 256)) ** -0.5, 3.0, ((0, 2), (1, 8))),
        "output_bias": noise(arg_keys[7], (D,), 0.5, 6.0, (), jnp.float32),
        "expand_weight": noise(arg_keys[8], (D, FF), D ** -0.5, 0.1875, ((0, 8), (1, 2))),
        "expand_bias": noise(arg_keys[9], (FF,), 0.5, 6.0, ((0, 2),), jnp.float32),
        "contract_weight": noise(arg_keys[10], (FF, D), (max(1, FF // 16)) ** -0.5, 0.375, ((0, 2), (1, 8))),
        "contract_bias": noise(arg_keys[11], (D,), 0.5, 6.0, (), jnp.float32),
        "cotangent": noise(arg_keys[12], (LATENTS, SEQ, D), 1.0, 6.0, ((0, 8), (1, 2))),
    }


EPS = 1e-06

def layer_norm(values):
    center = values - lax.optimization_barrier(jnp.mean(values, axis=-1, keepdims=True))
    inverse_std = lax.rsqrt(lax.optimization_barrier(jnp.mean(center * center, axis=-1, keepdims=True)) + EPS)
    return (center * inverse_std, inverse_std)

def norm_back(normed, inverse_std, upstream):
    return (upstream - lax.optimization_barrier(jnp.mean(upstream, axis=-1, keepdims=True)) - normed * lax.optimization_barrier(jnp.mean(upstream * normed, axis=-1, keepdims=True))) * inverse_std

def gelu_tanh(values):
    return jax.nn.gelu(values, approximate=True)

def gelu_back(before, upstream):
    return jax.vjp(gelu_tanh, before)[1](upstream)[0]

def silu_back(before, upstream):
    return jax.vjp(jax.nn.silu, before)[1](upstream)[0]

def reference(tokens, condition, ada_weight, ada_bias, qkv_weight, qv_bias, output_weight, output_bias, expand_weight, expand_bias, contract_weight, contract_bias, cotangent):
    f32 = jnp.float32
    bf16 = jnp.bfloat16
    score_scale = HD ** (-0.5)
    ada_flat = ada_weight.reshape(D, 6 * D)
    qkv_flat = qkv_weight.reshape(D, 3 * D)

    def latent_step(totals, sample):
        latent_tokens, latent_cond, latent_cot = sample
        squashed = jax.nn.silu(latent_cond.astype(f32)).astype(bf16)
        modulation = jnp.dot(squashed[None, :], ada_flat, preferred_element_type=f32).reshape(6, D) + ada_bias
        shift_one, scale_one, gate_one, shift_two, scale_two, gate_two = modulation
        stream = latent_tokens.astype(f32)
        normed_one, inverse_one = layer_norm(stream)
        shifted_one = (normed_one * (1.0 + scale_one) + shift_one).astype(bf16)
        projected = jnp.dot(shifted_one, qkv_flat, preferred_element_type=f32).reshape(SEQ, 3, D)
        queries = (projected[:, 0] + qv_bias[0]).astype(bf16).reshape(SEQ, HEADS, HD)
        keys_all = projected[:, 1].astype(bf16).reshape(SEQ, HEADS, HD)
        values_all = (projected[:, 2] + qv_bias[1]).astype(bf16).reshape(SEQ, HEADS, HD)
        scores = jnp.einsum('qhd,khd->hqk', queries.astype(f32), keys_all.astype(f32)) * score_scale
        top_score = lax.optimization_barrier(jnp.max(scores, axis=-1, keepdims=True))
        logsum = top_score + jnp.log(lax.optimization_barrier(jnp.sum(jnp.exp(scores - top_score), axis=-1, keepdims=True)))
        probs = jnp.exp(scores - logsum)
        probs_low = probs.astype(bf16)
        attended = jnp.einsum('hqk,khd->qhd', probs_low.astype(f32), values_all.astype(f32)).astype(bf16).reshape(SEQ, D)
        attn_out = jnp.dot(attended, output_weight, preferred_element_type=f32) + output_bias
        middle = stream + gate_one * attn_out
        normed_two, inverse_two = layer_norm(middle)
        shifted_two = (normed_two * (1.0 + scale_two) + shift_two).astype(bf16)
        hidden_pre = jnp.dot(shifted_two, expand_weight, preferred_element_type=f32) + expand_bias
        hidden_act = gelu_tanh(hidden_pre).astype(bf16)
        mlp_out = jnp.dot(hidden_act, contract_weight, preferred_element_type=f32) + contract_bias
        result = middle + gate_two * mlp_out
        upstream = latent_cot.astype(f32)
        grad_gate_two = lax.optimization_barrier(jnp.sum(upstream * mlp_out, axis=0))
        grad_mlp = upstream * gate_two
        bias_contract = lax.optimization_barrier(jnp.sum(grad_mlp, axis=0))
        mlp_low = grad_mlp.astype(bf16)
        weight_contract = jnp.dot(hidden_act.T, mlp_low, preferred_element_type=f32)
        grad_act = jnp.dot(mlp_low, contract_weight.T, preferred_element_type=f32)
        grad_pre = gelu_back(hidden_pre, grad_act)
        bias_expand = lax.optimization_barrier(jnp.sum(grad_pre, axis=0))
        pre_low = grad_pre.astype(bf16)
        weight_expand = jnp.dot(shifted_two.T, pre_low, preferred_element_type=f32)
        grad_shifted_two = jnp.dot(pre_low, expand_weight.T, preferred_element_type=f32)
        grad_scale_two = lax.optimization_barrier(jnp.sum(grad_shifted_two * normed_two, axis=0))
        grad_shift_two = lax.optimization_barrier(jnp.sum(grad_shifted_two, axis=0))
        grad_middle = upstream + norm_back(normed_two, inverse_two, grad_shifted_two * (1.0 + scale_two))
        grad_gate_one = lax.optimization_barrier(jnp.sum(grad_middle * attn_out, axis=0))
        grad_attn = grad_middle * gate_one
        bias_output = lax.optimization_barrier(jnp.sum(grad_attn, axis=0))
        attn_low = grad_attn.astype(bf16)
        weight_output = jnp.dot(attended.T, attn_low, preferred_element_type=f32)
        grad_attended = jnp.dot(attn_low, output_weight.T, preferred_element_type=f32).astype(bf16).reshape(SEQ, HEADS, HD)
        row_dot = jnp.einsum('qhd,qhd->hq', grad_attended.astype(f32), attended.reshape(SEQ, HEADS, HD).astype(f32))
        grad_probs = jnp.einsum('qhd,khd->hqk', grad_attended.astype(f32), values_all.astype(f32))
        grad_scores = (probs * (grad_probs - row_dot[..., None])).astype(bf16)
        grad_values = jnp.einsum('hqk,qhd->khd', probs_low.astype(f32), grad_attended.astype(f32))
        grad_queries = jnp.einsum('hqk,khd->qhd', grad_scores.astype(f32), keys_all.astype(f32)) * score_scale
        grad_keys = jnp.einsum('hqk,qhd->khd', grad_scores.astype(f32), queries.astype(f32)) * score_scale
        bias_qv = jnp.stack([lax.optimization_barrier(jnp.sum(grad_queries.reshape(SEQ, D), axis=0)), lax.optimization_barrier(jnp.sum(grad_values.reshape(SEQ, D), axis=0))])
        proj_low = jnp.stack([grad_queries.reshape(SEQ, D), grad_keys.reshape(SEQ, D), grad_values.reshape(SEQ, D)], axis=1).astype(bf16).reshape(SEQ, 3 * D)
        weight_qkv = jnp.dot(shifted_one.T, proj_low, preferred_element_type=f32).reshape(D, 3, D)
        grad_shifted_one = jnp.dot(proj_low, qkv_flat.T, preferred_element_type=f32)
        grad_scale_one = lax.optimization_barrier(jnp.sum(grad_shifted_one * normed_one, axis=0))
        grad_shift_one = lax.optimization_barrier(jnp.sum(grad_shifted_one, axis=0))
        grad_stream = grad_middle + norm_back(normed_one, inverse_one, grad_shifted_one * (1.0 + scale_one))
        grad_mod = jnp.stack([grad_shift_one, grad_scale_one, grad_gate_one, grad_shift_two, grad_scale_two, grad_gate_two])
        weight_ada = squashed.astype(f32)[:, None, None] * grad_mod[None, :, :]
        grad_squashed = jnp.dot(ada_flat.astype(f32), grad_mod.reshape(6 * D), precision=lax.Precision.HIGHEST)
        grad_cond = silu_back(latent_cond.astype(f32), grad_squashed)
        updates = (weight_ada, grad_mod, weight_qkv, bias_qv, weight_output, bias_output, weight_expand, bias_expand, weight_contract, bias_contract)
        totals = tuple((total + update for total, update in zip(totals, updates)))
        return (totals, (result, grad_stream, grad_cond))
    start = (jnp.zeros((D, 6, D), f32), jnp.zeros((6, D), f32), jnp.zeros((D, 3, D), f32), jnp.zeros((2, D), f32), jnp.zeros((D, D), f32), jnp.zeros((D,), f32), jnp.zeros((D, FF), f32), jnp.zeros((FF,), f32), jnp.zeros((FF, D), f32), jnp.zeros((D,), f32))
    totals, outputs = lax.scan(latent_step, start, (tokens, condition, cotangent))
    block_out, grad_tokens, grad_condition = outputs
    return (block_out, grad_tokens, grad_condition, totals[0], totals[1], totals[2], totals[3], totals[4], totals[5], totals[6], totals[7], totals[8], totals[9])
```

```python
import jax
import jax.numpy as jnp
from jax import lax
from jax.sharding import PartitionSpec as P

HD = 64
EPS = 1e-06
f32 = jnp.float32
bf16 = jnp.bfloat16
HIGHEST = lax.Precision.HIGHEST


def layer_norm(values):
    center = values - jnp.mean(values, axis=-1, keepdims=True)
    inverse_std = lax.rsqrt(jnp.mean(center * center, axis=-1, keepdims=True) + EPS)
    return (center * inverse_std, inverse_std)


def norm_back(normed, inverse_std, upstream):
    return (
        upstream
        - jnp.mean(upstream, axis=-1, keepdims=True)
        - normed * jnp.mean(upstream * normed, axis=-1, keepdims=True)
    ) * inverse_std


def gelu_tanh(values):
    return jax.nn.gelu(values, approximate=True)


def gelu_back(before, upstream):
    return jax.vjp(gelu_tanh, before)[1](upstream)[0]


def silu_back(before, upstream):
    return jax.vjp(jax.nn.silu, before)[1](upstream)[0]


def dot(a, b, contract, out=f32, precision=None):
    return lax.dot_general(
        a, b, ((contract[:1], contract[1:]), ((), ())), preferred_element_type=f32, precision=precision
    ).astype(out)


def body(
    tokens,
    condition,
    ada_weight,
    ada_bias,
    qkv_weight,
    qv_bias,
    output_weight,
    output_bias,
    expand_weight,
    expand_bias,
    contract_weight,
    contract_bias,
    cotangent,
):
    latents, own_rows, width = tokens.shape
    shards = lax.axis_size("shard")
    inner = 2 if shards % 2 == 0 else 1
    outer = shards // inner
    ctxs = lax.axis_size("ctx")
    tens = lax.axis_size("tensor")
    shard_at = lax.axis_index("shard")
    ctx_at = lax.axis_index("ctx")
    tensor_at = lax.axis_index("tensor")
    outer_at, inner_at = shard_at // inner, shard_at % inner
    blk = width // shards
    share = own_rows // tens
    cols_c = qkv_weight.shape[2]
    cols = cols_c // ctxs
    hid_c = expand_weight.shape[1]
    hid = hid_c // ctxs
    heads = cols // HD
    score_scale = HD ** (-0.5)

    def from_outer(v, k):
        pairs = [(s, ((s // inner - k) % outer) * inner + s % inner) for s in range(shards)]
        return lax.ppermute(v, "shard", pairs)

    def to_outer(v, k):
        return from_outer(v, -k)

    def flip(v):
        return lax.ppermute(v, "shard", [(s, s ^ 1) for s in range(shards)])

    def from_ctx(v, k):
        return lax.ppermute(v, "ctx", [(i, (i - k) % ctxs) for i in range(ctxs)])

    def from_core(v, k):
        return lax.ppermute(v, "tensor", [(i, (i - k) % tens) for i in range(tens)])

    def gather_shards(piece):
        parts = [piece] + [from_outer(piece, k) for k in range(1, outer)]
        if inner == 2:
            parts = parts + [flip(p) for p in parts]
        return parts

    def reduce_shards(low, high):
        rows = low.shape[0] // outer
        if inner == 2:
            low = low + flip(high.astype(bf16) if high.dtype == bf16 else high).astype(f32)
        own = low[:rows]
        for k in range(1, outer):
            piece = low[k * rows : (k + 1) * rows].astype(high.dtype)
            own = own + to_outer(piece, k).astype(f32)
        return own

    def gather_group(v):
        rows = jnp.concatenate([v] + [from_ctx(v, k) for k in range(1, ctxs)], axis=0)
        return jnp.concatenate([rows] + [from_core(rows, k) for k in range(1, tens)], axis=0)

    def reduce_group(first, rest):
        rows = ctxs * share
        total = first
        for k in range(1, tens):
            total = total + from_core(rest[(k - 1) * rows : k * rows], -k).astype(f32)
        own = total[:share]
        for k in range(1, ctxs):
            own = own + from_ctx(total[k * share : (k + 1) * share].astype(bf16), -k).astype(f32)
        return own

    rel = lax.broadcasted_iota(jnp.int32, (width, width), 1)
    row = lax.broadcasted_iota(jnp.int32, (width, width), 0)
    rel_blk = rel // blk
    rel_glob = (
        ((outer_at + rel_blk % outer) % outer) * inner + (inner_at + rel_blk // outer) % inner
    ) * blk + rel % blk
    order = row == rel_glob
    row_glob = ((tensor_at + row // cols_c) % tens) * cols_c + row % cols_c
    col_order = row_glob == rel_glob
    order_low = order.astype(bf16)
    order_f32 = order.astype(f32)
    col_order_f32 = col_order.astype(f32)

    def to_global(v):
        a = v.astype(bf16)
        left = v - a.astype(f32)
        b = left.astype(bf16)
        c = (left - b.astype(f32)).astype(bf16)
        return dot(a, order_low, (1, 1)) + dot(b, order_low, (1, 1)) + dot(c, order_low, (1, 1))

    cond_all = jnp.concatenate(gather_shards(condition), axis=0)
    squashed_all = jax.nn.silu(cond_all.astype(f32)).astype(bf16)
    squashed_rows = lax.dynamic_slice_in_dim(squashed_all, shard_at * blk, blk, 1)
    ada_flat = ada_weight.reshape(blk, 6 * cols_c)
    mod_part = dot(squashed_rows, ada_flat, (1, 0))
    half = mod_part.shape[0] // inner
    own_mod = reduce_shards(mod_part[:half], mod_part[half:]).reshape(latents * 6, cols_c)
    own_mod = own_mod + jnp.tile(ada_bias, (latents, 1))
    mod_cols = jnp.concatenate([own_mod] + [from_core(own_mod, k) for k in range(1, tens)], axis=1)
    modulation = dot(mod_cols, col_order_f32, (1, 0), precision=HIGHEST).reshape(latents, 6, width)

    def per_row(v, count):
        return v[:, None, :] if count is None else jnp.broadcast_to(v[:, None, :], (latents, count, width))

    def latent_rows(v, blocks):
        if latents == 1:
            return v
        return jnp.tile(jnp.repeat(v, share, axis=0), (blocks, 1))

    blocks = ctxs * tens
    rows_own = latents * share
    del per_row

    def ctx_cols(v, size, axis):
        return lax.dynamic_slice_in_dim(v, ctx_at * size, size, axis)

    qkv_piece = ctx_cols(qkv_weight, cols, 2).reshape(blk, 3 * cols)
    out_piece = ctx_cols(output_weight, cols, 0).T
    expand_piece = ctx_cols(expand_weight, hid, 1)
    contract_piece = ctx_cols(contract_weight, hid, 0).T
    qkv_full = jnp.concatenate(gather_shards(qkv_piece), axis=0)
    rest_full = jnp.concatenate(
        gather_shards(jnp.concatenate([out_piece, expand_piece, contract_piece], axis=1)), axis=0
    )
    out_t = rest_full[:, :cols]
    expand_full = rest_full[:, cols : cols + hid]
    contract_t = rest_full[:, cols + hid :]

    biases = dot(jnp.stack([output_bias, contract_bias]), order_f32, (1, 0), precision=HIGHEST)
    out_bias, con_bias = biases[0:1], biases[1:2]
    qv_own = ctx_cols(qv_bias, cols, 1)
    expand_own = ctx_cols(expand_bias, hid, 0)

    def group_rows(v):
        mine = lax.dynamic_slice_in_dim(v, tensor_at * share, share, 1).reshape(rows_own, width)
        return gather_group(dot(mine, order_low, (1, 0), bf16))

    tok = group_rows(tokens)
    cot = group_rows(cotangent)
    share = rows_own
    all_rows = blocks * rows_own

    def mod_of(i, count):
        return latent_rows(modulation[:, i], count)

    stream = tok.astype(f32)
    normed_one, inverse_one = layer_norm(stream)
    shifted_one = (normed_one * (1.0 + mod_of(1, blocks)) + mod_of(0, blocks)).astype(bf16)
    projected = dot(shifted_one, qkv_full, (1, 0))

    def split_heads(v):
        return v.reshape(blocks, latents, share // latents, heads, HD)

    q_low = (projected[:, :cols] + qv_own[0]).astype(bf16)
    k_low = projected[:, cols : 2 * cols].astype(bf16)
    v_low = (projected[:, 2 * cols :] + qv_own[1]).astype(bf16)

    def heads_first(v):
        per_latent = v.reshape(blocks, latents, share // latents, heads, HD)
        return per_latent.transpose(1, 3, 0, 2, 4).reshape(latents * heads, blocks * (share // latents), HD)

    def heads_last(v):
        back = v.reshape(latents, heads, blocks, share // latents, HD).transpose(2, 0, 3, 1, 4)
        return back.reshape(all_rows, cols)

    queries, keys, values = heads_first(q_low), heads_first(k_low), heads_first(v_low)
    scores = jnp.einsum("hqd,hkd->hqk", queries, keys, preferred_element_type=f32) * score_scale
    top_score = jnp.max(scores, axis=-1, keepdims=True)
    logsum = top_score + jnp.log(jnp.sum(jnp.exp(scores - top_score), axis=-1, keepdims=True))
    probs_low = jnp.exp(scores - logsum).astype(bf16)
    attended_h = jnp.einsum("hqk,hkd->hqd", probs_low, values, preferred_element_type=f32).astype(bf16)
    attended = heads_last(attended_h)

    own_block = ctxs * share

    def group_product(a, b, contract):
        first = dot(a[:own_block], b, contract)
        rest = dot(a[own_block:], b, contract, bf16)
        return reduce_group(first, rest)

    attn_share = group_product(attended, out_t, (1, 1)) + out_bias
    gate_one, gate_two = mod_of(2, 1), mod_of(5, 1)
    middle_share = stream[:share] + gate_one * attn_share
    normed_two, inverse_two = layer_norm(middle_share)
    shifted_two = gather_group((normed_two * (1.0 + mod_of(4, 1)) + mod_of(3, 1)).astype(bf16))
    hidden_pre = dot(shifted_two, expand_full, (1, 0)) + expand_own
    hidden_act = gelu_tanh(hidden_pre).astype(bf16)
    mlp_share = group_product(hidden_act, contract_t, (1, 1)) + con_bias
    result_share = middle_share + gate_two * mlp_share

    def latent_sum(v):
        return jnp.sum(v.reshape(latents, -1, width), axis=1)

    def latent_sum_all(v):
        return jnp.sum(v.reshape(blocks, latents, -1, width), axis=(0, 2))

    def weight_grad(a, g):
        n = width // inner
        low = dot(a[:, :n], g, (0, 0))
        high = dot(a[:, n:], g, (0, 0), bf16)
        return reduce_shards(low, high)

    upstream_share = cot[:share].astype(f32)
    mlp_low = (cot.astype(f32) * mod_of(5, blocks)).astype(bf16)
    owned_contract = weight_grad(mlp_low, hidden_act)
    grad_act = dot(mlp_low, contract_t, (1, 0))
    grad_pre = gelu_back(hidden_pre, grad_act)
    bias_expand = jnp.sum(grad_pre, axis=0)
    pre_low = grad_pre.astype(bf16)
    grad_shifted_two = group_product(pre_low, expand_full, (1, 1))
    owned_expand = weight_grad(shifted_two, pre_low)
    grad_gate_two = latent_sum(upstream_share * mlp_share)
    bias_contract = jnp.sum(upstream_share * gate_two, axis=0)
    grad_scale_two = latent_sum(grad_shifted_two * normed_two)
    grad_shift_two = latent_sum(grad_shifted_two)
    middle_grad = upstream_share + norm_back(
        normed_two, inverse_two, grad_shifted_two * (1.0 + mod_of(4, 1))
    )
    grad_gate_one = latent_sum(middle_grad * attn_share)
    grad_attn = middle_grad * gate_one
    bias_output = jnp.sum(grad_attn, axis=0)
    attn_low = gather_group(grad_attn.astype(bf16))
    grad_attended = dot(attn_low, out_t, (1, 0), bf16)
    owned_output = weight_grad(attn_low, attended)
    grad_attended_h = heads_first(grad_attended)
    row_dot = jnp.sum(grad_attended_h.astype(f32) * attended_h.astype(f32), axis=-1, keepdims=True)
    probs = jnp.exp(scores - logsum)
    grad_probs = jnp.einsum("hqd,hkd->hqk", grad_attended_h, values, preferred_element_type=f32)
    grad_scores = (probs * (grad_probs - row_dot)).astype(bf16)
    grad_values = jnp.einsum("hqk,hqd->hkd", probs_low, grad_attended_h, preferred_element_type=f32)
    grad_queries = jnp.einsum("hqk,hkd->hqd", grad_scores, keys, preferred_element_type=f32) * score_scale
    grad_keys = jnp.einsum("hqk,hqd->hkd", grad_scores, queries, preferred_element_type=f32) * score_scale

    def head_bias(v):
        return jnp.sum(v.reshape(latents, heads, -1, HD), axis=(0, 2)).reshape(cols)

    bias_qv = jnp.stack([head_bias(grad_queries), head_bias(grad_values)])
    proj_low = jnp.concatenate(
        [heads_last(v.astype(bf16)) for v in (grad_queries, grad_keys, grad_values)], axis=1
    )
    first_low = dot(proj_low[:own_block], qkv_full, (1, 1))
    rest_f32 = dot(proj_low[own_block:], qkv_full, (1, 1))
    first_part = jnp.concatenate([first_low, rest_f32], axis=0)
    part_scale = latent_sum_all(first_part * normed_one)
    part_shift = latent_sum_all(first_part)
    owned_qkv = weight_grad(shifted_one, proj_low)
    grad_shifted_one = reduce_group(first_low, rest_f32.astype(bf16))
    grad_stream = middle_grad + norm_back(
        normed_one[:share], inverse_one[:share], grad_shifted_one * (1.0 + mod_of(1, 1))
    )

    def token_out(v):
        v = to_global(v).reshape(latents, -1, width)
        n = v.shape[1]
        out = jnp.zeros((latents, own_rows, width), f32)
        for k in range(tens):
            piece = v if k == 0 else from_core(v, k)
            out = lax.dynamic_update_slice_in_dim(out, piece, ((tensor_at + k) % tens) * n, 1)
        return out

    result = token_out(result_share)
    grad_tokens = token_out(grad_stream)

    grad_mod = jnp.stack(
        [part_shift, part_scale, grad_gate_one, grad_shift_two, grad_scale_two, grad_gate_two], axis=1
    ).reshape(latents * 6, width)
    packet = jnp.concatenate([grad_mod, bias_output[None], bias_contract[None]], axis=0)
    packet = dot(packet, col_order_f32, (1, 1), precision=HIGHEST)
    total = packet[:, :cols_c]
    for k in range(1, tens):
        total = total + from_core(packet[:, k * cols_c : (k + 1) * cols_c], -k)
    side = jnp.concatenate([bias_qv.reshape(-1), bias_expand])
    flat = jnp.concatenate([total.reshape(-1), side])
    summed = total
    qv_pad = jnp.zeros((2, cols_c), f32)
    expand_pad = jnp.zeros((hid_c,), f32)
    n_total = total.size
    for k in range(ctxs):
        got = flat if k == 0 else from_ctx(flat, k)
        at = (ctx_at + k) % ctxs
        if k:
            summed = summed + got[:n_total].reshape(total.shape)
        qv_pad = lax.dynamic_update_slice_in_dim(
            qv_pad, got[n_total : n_total + 2 * cols].reshape(2, cols), at * cols, 1
        )
        expand_pad = lax.dynamic_update_slice_in_dim(expand_pad, got[n_total + 2 * cols :], at * hid, 0)
    message = jnp.concatenate([summed.reshape(-1), qv_pad.reshape(-1), expand_pad])[None]
    gathered = jnp.concatenate(gather_shards(message), axis=0)
    n_mod = latents * 6 * cols_c
    mod_all = gathered[:, :n_mod].reshape(shards * latents, 6 * cols_c)
    sums = jnp.sum(gathered[:, n_mod:], axis=0)
    out_cols, con_cols = sums[:cols_c], sums[cols_c : 2 * cols_c]
    grad_qv_bias = sums[2 * cols_c : 4 * cols_c].reshape(2, cols_c)
    grad_expand_bias = sums[4 * cols_c :]
    grad_ada_bias = jnp.sum(mod_all, axis=0).reshape(6, cols_c)
    own_cols = blk // ctxs
    squashed_own = lax.dynamic_slice_in_dim(squashed_all, (shard_at * ctxs + ctx_at) * own_cols, own_cols, 1)
    grad_ada = dot(squashed_own.astype(f32), mod_all, (0, 0), precision=HIGHEST).reshape(own_cols, 6, cols_c)
    cond_part = dot(mod_all, ada_flat.astype(f32), (1, 1), precision=HIGHEST)
    tail = jnp.concatenate([cond_part.reshape(-1), out_cols, con_cols])
    n_cond = cond_part.size
    cond_sum = cond_part
    vectors = jnp.zeros((2, width), f32)
    for k in range(tens):
        got = tail if k == 0 else from_core(tail, k)
        if k:
            cond_sum = cond_sum + got[:n_cond].reshape(cond_part.shape)
        vectors = lax.dynamic_update_slice_in_dim(
            vectors, got[n_cond:].reshape(2, cols_c), ((tensor_at + k) % tens) * cols_c, 1
        )
    half = cond_sum.shape[0] // inner
    parts = [cond_sum[:half].reshape(outer, latents, 1, blk)]
    if inner == 2:
        parts.append(flip(cond_sum[half:]).reshape(outer, latents, 1, blk))
    both = jnp.concatenate(parts, axis=2)
    grad_squashed = jnp.zeros((latents, width), f32)
    for k in range(outer):
        got = both[k] if k == 0 else to_outer(both[k], k)
        for j in range(inner):
            at = (((outer_at - k) % outer) * inner + (inner_at + j) % inner) * blk
            grad_squashed = lax.dynamic_update_slice_in_dim(grad_squashed, got[:, j], at, 1)
    grad_cond = silu_back(condition.astype(f32), grad_squashed)

    def to_owner(v, names, parts):
        rows = blk // ctxs
        n = v.shape[1] // parts
        v = v.reshape(blk, parts, n)
        out = jnp.zeros((rows, parts, n * ctxs), f32)
        for k in range(ctxs):
            to = (ctx_at - k) % ctxs
            piece = lax.dynamic_slice_in_dim(v, to * rows, rows, 0)
            if k:
                piece = from_ctx(piece.astype(bf16), k).astype(f32)
            out = lax.dynamic_update_slice_in_dim(out, piece, ((ctx_at + k) % ctxs) * n, 2)
        return out

    grad_qkv = to_owner(owned_qkv, "qkv", 3)
    grad_expand = to_owner(owned_expand, "expand", 1)[:, 0]
    grad_output = to_owner(owned_output, "output", 1)[:, 0].T
    grad_contract = to_owner(owned_contract, "contract", 1)[:, 0].T
    return (
        result,
        grad_tokens,
        grad_cond,
        grad_ada,
        grad_ada_bias,
        grad_qkv,
        grad_qv_bias,
        grad_output,
        vectors[0],
        grad_expand,
        grad_expand_bias,
        grad_contract,
        vectors[1],
    )


def solution(mesh):
    in_specs = (
        P("shard", "ctx", None),
        P("shard", None),
        P("shard", None, "tensor"),
        P(None, "tensor"),
        P("shard", None, "tensor"),
        P(None, "tensor"),
        P("tensor", "shard"),
        P(),
        P("shard", "tensor"),
        P("tensor"),
        P("tensor", "shard"),
        P(),
        P("shard", "ctx", None),
    )
    out_specs = (
        P("shard", "ctx", None),
        P("shard", "ctx", None),
        P("shard", None),
        P(("shard", "ctx"), None, "tensor"),
        P(None, "tensor"),
        P(("shard", "ctx"), None, "tensor"),
        P(None, "tensor"),
        P("tensor", ("shard", "ctx")),
        P(),
        P(("shard", "ctx"), "tensor"),
        P("tensor"),
        P("tensor", ("shard", "ctx")),
        P(),
    )
    return jax.shard_map(body, mesh=mesh, in_specs=in_specs, out_specs=out_specs, check_vma=False)
```

```python
import jax
import jax.numpy as jnp
from jax import lax
from jax.experimental import pallas as pl
from jax.experimental.pallas import tpu as pltpu
from jax.sharding import PartitionSpec as P

HD = 64
EPS = 1e-06
f32 = jnp.float32
bf16 = jnp.bfloat16
HIGHEST = lax.Precision.HIGHEST


def layer_norm(values):
    center = values - jnp.mean(values, axis=-1, keepdims=True)
    inverse_std = lax.rsqrt(jnp.mean(center * center, axis=-1, keepdims=True) + EPS)
    return (center * inverse_std, inverse_std)


def norm_back(normed, inverse_std, upstream):
    return (
        upstream
        - jnp.mean(upstream, axis=-1, keepdims=True)
        - normed * jnp.mean(upstream * normed, axis=-1, keepdims=True)
    ) * inverse_std


def gelu_tanh(values):
    return jax.nn.gelu(values, approximate=True)


def gelu_back(before, upstream):
    return jax.vjp(gelu_tanh, before)[1](upstream)[0]


def silu_back(before, upstream):
    return jax.vjp(jax.nn.silu, before)[1](upstream)[0]


def dot(a, b, contract, out=f32, precision=None):
    return lax.dot_general(
        a, b, ((contract[:1], contract[1:]), ((), ())), preferred_element_type=f32, precision=precision
    ).astype(out)


def _nt(a, b):
    return lax.dot_general(a, b, (((1,), (1,)), ((), ())), preferred_element_type=f32)


def _nn(a, b):
    return lax.dot_general(a, b, (((1,), (0,)), ((), ())), preferred_element_type=f32)


def _loop(rows, chunk, step):
    if rows == chunk:
        step(slice(0, rows))
        return

    def one(c, carry):
        step(pl.ds(pl.multiple_of(c * chunk, chunk), chunk))
        return carry

    lax.fori_loop(0, rows // chunk, one, 0)


def project_kernel(chunk, count, *refs):
    tok_ref, shift_ref, scale_ref, bias_ref = refs[:4]
    pieces, (low_ref, shifted_ref, weight_ref) = refs[4 : 4 + count], refs[4 + count :]
    n = weight_ref.shape[0] // count
    for p, piece in enumerate(pieces):
        weight_ref[p * n : (p + 1) * n, :] = piece[...]
    gain = 1.0 + scale_ref[...]

    def step(at):
        normed, _ = layer_norm(tok_ref[at, :].astype(f32))
        shifted = (normed * gain + shift_ref[...]).astype(bf16)
        shifted_ref[at, :] = shifted
        low_ref[at, :] = (_nn(shifted, weight_ref[...]) + bias_ref[...]).astype(bf16)

    _loop(tok_ref.shape[0], chunk, step)


def assemble_kernel(*refs):
    out_ref = refs[-1]
    n, half = refs[0].shape[0] // 2, out_ref.shape[0] // 2
    for p, ref in enumerate(refs[:-1]):
        out_ref[p * n : (p + 1) * n, :] = ref[:n, :]
        out_ref[half + p * n : half + (p + 1) * n, :] = ref[n:, :]


def assemble(pairs):
    rows, columns = pairs[0].shape
    return pl.pallas_call(
        assemble_kernel,
        out_shape=jax.ShapeDtypeStruct((rows * len(pairs), columns), bf16),
        cost_estimate=_CHEAP,
        name="assemble",
    )(*pairs)


def project(tok, shift, scale, bias, pieces):
    rows, width = tok.shape
    columns = pieces[0].shape[1]
    return pl.pallas_call(
        lambda *refs: project_kernel(_chunk(rows), len(pieces), *refs),
        out_shape=[
            jax.ShapeDtypeStruct((rows, columns), bf16),
            jax.ShapeDtypeStruct((rows, width), bf16),
            jax.ShapeDtypeStruct((width, columns), bf16),
        ],
        cost_estimate=_CHEAP,
        name="project",
    )(tok, shift, scale, bias, *pieces)


def attend_kernel(chunk, q_ref, k_ref, v_ref, out_ref, stat_ref):
    rows, lanes = out_ref.shape
    heads = [slice(h * HD, (h + 1) * HD) for h in range(lanes // HD)]
    values_t = v_ref[...].T

    def step(at):
        outs = []
        for h, lane in enumerate(heads):
            queries = q_ref[at, lane] * bf16(HD**-0.5)
            scores = _nt(k_ref[:, lane], queries)
            top = jnp.max(scores, axis=0, keepdims=True)
            logsum = top + jnp.log(jnp.sum(jnp.exp(scores - top), axis=0, keepdims=True))
            probs = jnp.exp(scores - logsum).astype(bf16)
            outs.append(_nn(values_t[lane, :], probs))
            stat_ref[h : h + 1, at] = logsum
        out_ref[at, :] = jnp.concatenate(outs, axis=0).T.astype(bf16)

    _loop(rows, chunk, step)


def attend_back_kernel(
    chunk,
    steps,
    q_ref,
    k_ref,
    v_ref,
    grad_ref,
    out_ref,
    stat_ref,
    proj_ref,
    bias_ref,
    keys_acc,
    values_acc,
):
    rows, lanes = out_ref.shape
    scale = HD**-0.5
    heads = [slice(h * HD, (h + 1) * HD) for h in range(lanes // HD)]

    def columns(part):
        if steps == 1:
            return slice(part * lanes, (part + 1) * lanes)
        return pl.ds(pl.multiple_of((part * steps + pl.program_id(0)) * lanes, lanes), lanes)

    keys_t = k_ref[...].T
    keys_acc[...] = jnp.zeros_like(keys_acc)
    values_acc[...] = jnp.zeros_like(values_acc)
    bias_ref[...] = jnp.zeros_like(bias_ref)

    def step(at):
        grad_queries, grad_keys, grad_values = [], [], []
        product = (grad_ref[at, :].astype(f32) * out_ref[at, :].astype(f32)).T
        for h, lane in enumerate(heads):
            queries, grad = q_ref[at, lane], grad_ref[at, lane]
            row_dot = jnp.sum(product[lane, :], axis=0, keepdims=True)
            probs = jnp.exp(_nt(k_ref[:, lane], queries * bf16(scale)) - stat_ref[h : h + 1, at])
            grad_scores = (probs * (_nt(v_ref[:, lane], grad) - row_dot)).astype(bf16)
            grad_values.append(_nn(probs.astype(bf16), grad))
            grad_keys.append(_nn(grad_scores, queries))
            grad_queries.append(_nn(keys_t[lane, :], grad_scores))
        values_acc[...] += jnp.concatenate(grad_values, axis=1)
        keys_acc[...] += jnp.concatenate(grad_keys, axis=1)
        got = jnp.concatenate(grad_queries, axis=0).T * scale
        bias_ref[0:1, :] += jnp.sum(got, axis=0, keepdims=True)
        proj_ref[at, columns(0)] = got.astype(bf16)

    _loop(rows, chunk, step)
    proj_ref[:, columns(1)] = (keys_acc[...] * scale).astype(bf16)
    proj_ref[:, columns(2)] = values_acc[...].astype(bf16)
    bias_ref[1:2, :] = jnp.sum(values_acc[...], axis=0, keepdims=True)


def _chunk(rows):
    return 256 if rows % 256 == 0 else rows


_CHEAP = pl.CostEstimate(flops=1000, bytes_accessed=1000, transcendentals=0)


def _parts(qkv, lanes, steps):
    if steps == 1:
        arrays = [qkv[:, j * lanes : (j + 1) * lanes] for j in range(3)]
        return arrays, [pl.BlockSpec((qkv.shape[0], lanes), lambda i: (0, 0))] * 3
    specs = [
        pl.BlockSpec((qkv.shape[0], lanes), lambda i, j=j: (0, j * steps + i)) for j in range(3)
    ]
    return [qkv] * 3, specs


def attend(qkv, lanes):
    rows, steps = qkv.shape[0], qkv.shape[1] // (3 * lanes)
    parts, specs = _parts(qkv, lanes, steps)
    return pl.pallas_call(
        lambda *refs: attend_kernel(_chunk(rows), *refs),
        grid=(steps,),
        in_specs=specs,
        out_specs=[
            pl.BlockSpec((rows, lanes), lambda i: (0, i)),
            pl.BlockSpec((8, rows), lambda i: (i, 0)),
        ],
        out_shape=[
            jax.ShapeDtypeStruct((rows, steps * lanes), bf16),
            jax.ShapeDtypeStruct((8 * steps, rows), f32),
        ],
        cost_estimate=_CHEAP,
        name="attend",
    )(*parts)


def attend_back(qkv, grad, out, stat, lanes):
    rows, steps = qkv.shape[0], qkv.shape[1] // (3 * lanes)
    parts, specs = _parts(qkv, lanes, steps)
    own = pl.BlockSpec((rows, lanes), lambda i: (0, i))
    return pl.pallas_call(
        lambda *refs: attend_back_kernel(_chunk(rows), steps, *refs),
        grid=(steps,),
        in_specs=[
            *specs, own, own, pl.BlockSpec((8, rows), lambda i: (i, 0))
        ],
        out_specs=[
            pl.BlockSpec((rows, 3 * steps * lanes), lambda i: (0, 0)),
            pl.BlockSpec((8, lanes), lambda i: (i, 0)),
        ],
        out_shape=[
            jax.ShapeDtypeStruct((rows, 3 * steps * lanes), bf16),
            jax.ShapeDtypeStruct((8 * steps, lanes), f32),
        ],
        cost_estimate=_CHEAP,
        scratch_shapes=[pltpu.VMEM((rows, lanes), f32)] * 2,
        name="attend_back",
    )(*parts, grad, out, stat)


def layer(
    tokens,
    condition,
    ada_weight,
    ada_bias,
    qkv_weight,
    qv_bias,
    output_weight,
    output_bias,
    expand_weight,
    expand_bias,
    contract_weight,
    contract_bias,
    cotangent,
):
    latents, own_rows, width = tokens.shape
    shards = lax.axis_size("shard")
    ctxs = lax.axis_size("ctx")
    tens = lax.axis_size("tensor")
    shard_at = lax.axis_index("shard")
    ctx_at = lax.axis_index("ctx")
    tensor_at = lax.axis_index("tensor")
    blk = width // shards
    share = own_rows // tens
    cols_c = qkv_weight.shape[2]
    cols = cols_c // ctxs
    hid_c = expand_weight.shape[1]
    hid = hid_c // ctxs

    bits = shards.bit_length() - 1
    assert shards == 1 << bits

    def mask_of(place):
        return sum(((place >> i) & 1) << (bits - 1 - i) for i in range(bits))

    def swap(v, mask):
        return lax.ppermute(v, "shard", [(s, s ^ mask) for s in range(shards)])

    def tie(v, *after):
        return lax.optimization_barrier((v, *after))[0]

    def from_ctx(v, k):
        return lax.ppermute(v, "ctx", [(i, (i - k) % ctxs) for i in range(ctxs)])

    def from_core(v, k):
        return lax.ppermute(v, "tensor", [(i, (i - k) % tens) for i in range(tens)])

    def gather_half(piece):
        parts = [piece]
        for p in range(1, shards // 2):
            parts.append(swap(piece, mask_of(p)))
        return parts

    def gather_direct(piece):
        n = shards // 2
        parts = [piece] * shards
        parts[n] = swap(piece, 1)
        for p in sorted(range(1, n), key=mask_of):
            parts[p] = swap(piece, mask_of(p))
            parts[n + p] = swap(parts[p], 1)
        return parts

    def gather_shards(piece, *after):
        parts = gather_half(piece)
        if after:
            parts = lax.optimization_barrier((*parts, *after))[: len(parts)]
        half = lax.optimization_barrier(jnp.concatenate(parts, axis=0))
        other = swap(half, 1)
        return lambda *late: jnp.concatenate([half, tie(other, *late) if late else other], axis=0)

    def pair_of(piece):
        return jnp.concatenate([piece, swap(piece, 1)], axis=0)

    def gather_pairs(pair, *late):
        got = [swap(pair, mask_of(p)) for p in range(1, shards // 2)]
        got = lax.optimization_barrier((*got, *late))[: len(got)]
        return assemble([pair, *got])

    def reduce_shards(low, high, *after):
        kind = high.dtype
        got = swap(high, 1)
        if after:
            got = tie(got, *after)
        n = low.shape[0] // (shards // 2)
        own = low[:n] + got[:n].astype(f32)
        sent = [
            (low[p * n : (p + 1) * n] + got[p * n : (p + 1) * n].astype(f32)).astype(kind)
            for p in range(1, shards // 2)
        ]
        pieces = []
        for p, piece in zip(range(1, shards // 2), sent):
            pieces.append(swap(piece, mask_of(p)))

        def total(*late):
            parts = lax.optimization_barrier((*pieces, *late))[: len(pieces)] if late else pieces
            return sum((v.astype(f32) for v in parts), own)

        return total

    def gather_group(v, *late):
        rows = [from_ctx(v, k) for k in range(1, ctxs)]
        rows = [v] + [tie(r, *late) if late else r for r in rows]
        rows = jnp.concatenate(rows, axis=0)
        others = [from_core(rows, k) for k in range(1, tens)]
        return jnp.concatenate([rows] + others, axis=0)

    def reduce_cores(first, rest):
        rows = ctxs * share
        total = first
        for k in range(1, tens):
            got = from_core(rest[(k - 1) * rows : k * rows], -k)
            total = total + got.astype(f32)
        return total

    def reduce_ctx(total, *late):
        own = total[:share]
        for k in range(1, ctxs):
            piece = total[k * share : (k + 1) * share].astype(bf16)
            got = from_ctx(piece, -k)
            own = own + (tie(got, *late) if late else got).astype(f32)
        return own

    rel = lax.broadcasted_iota(jnp.int32, (width, width), 1)
    row = lax.broadcasted_iota(jnp.int32, (width, width), 0)
    rel_blk = rel // blk
    rel_mask = sum(((rel_blk >> i) & 1) << (bits - 1 - i) for i in range(bits))
    rel_glob = (shard_at ^ rel_mask) * blk + rel % blk
    order = row == rel_glob
    row_glob = ((tensor_at + row // cols_c) % tens) * cols_c + row % cols_c
    col_order = row_glob == rel_glob
    order_low = order.astype(bf16)
    order_f32 = order.astype(f32)
    col_order_f32 = col_order.astype(f32)

    def to_global(v):
        a = v.astype(bf16)
        left = v - a.astype(f32)
        b = left.astype(bf16)
        c = (left - b.astype(f32)).astype(bf16)
        return dot(a, order_low, (1, 1)) + dot(b, order_low, (1, 1)) + dot(c, order_low, (1, 1))

    cond_all = gather_shards(condition)()
    squashed_all = jax.nn.silu(cond_all.astype(f32)).astype(bf16)
    squashed_rows = lax.dynamic_slice_in_dim(squashed_all, shard_at * blk, blk, 1)
    ada_flat = ada_weight.reshape(blk, 6 * cols_c)
    mod_part = dot(squashed_rows, ada_flat, (1, 0))
    half = mod_part.shape[0] // 2
    mod_sum = reduce_shards(mod_part[:half], mod_part[half:])()
    own_mod = mod_sum.reshape(latents * 6, cols_c)
    own_mod = own_mod + jnp.tile(ada_bias, (latents, 1))
    mod_cols = jnp.concatenate([own_mod] + [from_core(own_mod, k) for k in range(1, tens)], axis=1)
    modulation = dot(mod_cols, col_order_f32, (1, 0), precision=HIGHEST).reshape(latents, 6, width)

    def per_row(v, count):
        return v[:, None, :] if count is None else jnp.broadcast_to(v[:, None, :], (latents, count, width))

    def latent_rows(v, blocks):
        if latents == 1:
            return v
        return jnp.tile(jnp.repeat(v, share, axis=0), (blocks, 1))

    blocks = ctxs * tens
    rows_own = latents * share
    del per_row

    def ctx_cols(v, size, axis):
        return lax.dynamic_slice_in_dim(v, ctx_at * size, size, axis)

    lanes = min(cols, 2 * HD)
    steps = cols // lanes

    qkv_piece = ctx_cols(qkv_weight, cols, 2).reshape(blk, 3 * cols)
    out_piece = ctx_cols(output_weight, cols, 0).T
    expand_piece = ctx_cols(expand_weight, hid, 1)
    contract_piece = ctx_cols(contract_weight, hid, 0).T
    qkv_parts = gather_direct(qkv_piece)
    biases = dot(jnp.stack([output_bias, contract_bias]), order_f32, (1, 0), precision=HIGHEST)
    out_bias, con_bias = biases[0:1], biases[1:2]
    qv_own = ctx_cols(qv_bias, cols, 1)
    expand_own = ctx_cols(expand_bias, hid, 0)

    def own_rows_of(v):
        mine = lax.dynamic_slice_in_dim(v, tensor_at * share, share, 1).reshape(rows_own, width)
        return dot(mine, order_low, (1, 0), bf16)

    tok = gather_group(own_rows_of(tokens), mod_sum)
    cot_own = own_rows_of(cotangent)
    share = rows_own

    def mod_of(i, count):
        return latent_rows(modulation[:, i], count)

    stream = tok[:share].astype(f32)
    qkv_bias = jnp.concatenate([qv_own[0], jnp.zeros((cols,), f32), qv_own[1]])[None]
    contract_pair = pair_of(contract_piece)
    qkv_low, shifted_one, qkv_full = project(
        tok, modulation[:, 0], modulation[:, 1], qkv_bias, qkv_parts
    )
    cot = gather_group(cot_own, qkv_low)
    out_t = gather_shards(out_piece, qkv_low)()
    attended, stat = attend(qkv_low, lanes)
    expand_full = gather_shards(expand_piece, attended)()
    own_block = ctxs * share

    def core_product(a, b, contract):
        rest = dot(a[own_block:], b, contract, bf16)
        first = dot(a[:own_block], b, contract)
        return reduce_cores(first, rest)

    attn_core = core_product(attended, out_t, (1, 1))
    attn_share = reduce_ctx(attn_core) + out_bias
    gate_one, gate_two = mod_of(2, 1), mod_of(5, 1)
    middle_share = stream + gate_one * attn_share
    normed_two, inverse_two = layer_norm(middle_share)
    shifted_two = gather_group((normed_two * (1.0 + mod_of(4, 1)) + mod_of(3, 1)).astype(bf16))
    hidden_pre = dot(shifted_two, expand_full, (1, 0)) + expand_own
    hidden_act = gelu_tanh(hidden_pre).astype(bf16)
    contract_t = gather_pairs(contract_pair, hidden_act)

    def latent_sum(v):
        return jnp.sum(v.reshape(latents, -1, width), axis=1)

    def latent_sum_all(v):
        return jnp.sum(v.reshape(blocks, latents, -1, width), axis=(0, 2))

    def grad_high(a, g):
        return dot(a[:, width // 2 :], g, (0, 0), bf16)

    def grad_low(a, g):
        return dot(a[:, : width // 2], g, (0, 0))

    upstream_share = cot[:share].astype(f32)
    mlp_low = (cot.astype(f32) * mod_of(5, blocks)).astype(bf16)
    contract_high = grad_high(mlp_low, hidden_act)
    grad_act = dot(tie(mlp_low, contract_high), contract_t, (1, 0))
    grad_pre = gelu_back(hidden_pre, grad_act)
    bias_expand = jnp.sum(grad_pre, axis=0)
    pre_low = grad_pre.astype(bf16)
    two_core = core_product(pre_low, expand_full, (1, 1))
    grad_shifted_two = reduce_ctx(two_core)
    normed_one, inverse_one = layer_norm(tie(tok, two_core).astype(f32))
    bias_contract = jnp.sum(upstream_share * gate_two, axis=0)
    grad_scale_two = latent_sum(grad_shifted_two * normed_two)
    grad_shift_two = latent_sum(grad_shifted_two)
    middle_grad = upstream_share + norm_back(
        normed_two, inverse_two, grad_shifted_two * (1.0 + mod_of(4, 1))
    )
    grad_gate_one = latent_sum(middle_grad * attn_share)
    grad_attn = middle_grad * gate_one
    bias_output = jnp.sum(grad_attn, axis=0)
    low_share = grad_attn.astype(bf16)
    attn_low = gather_group(low_share)
    grad_attended = dot(attn_low, out_t, (1, 0), bf16)
    proj_low, bias_heads = attend_back(qkv_low, grad_attended, attended, stat, lanes)
    bias_heads = bias_heads.reshape(steps, 8, lanes)
    bias_qv = jnp.stack([bias_heads[:, 0].reshape(cols), bias_heads[:, 1].reshape(cols)])
    pre_late = tie(pre_low, two_core)
    expand_high = grad_high(shifted_two, pre_late)
    output_high = grad_high(attn_low, attended)
    mlp_core = core_product(tie(hidden_act, two_core), contract_t, (1, 1))
    owned_contract = reduce_shards(
        grad_low(mlp_low, tie(hidden_act, two_core)), contract_high, low_share
    )
    owned_expand = reduce_shards(grad_low(shifted_two, pre_late), expand_high, proj_low)
    mlp_share = reduce_ctx(mlp_core, proj_low) + con_bias
    result_share = middle_share + gate_two * mlp_share
    grad_gate_two = latent_sum(upstream_share * mlp_share)
    qkv_high = jnp.concatenate([grad_high(shifted_one, proj_low), output_high], axis=1)
    proj_late = tie(proj_low, qkv_high)
    rest_f32 = dot(proj_late[own_block:], qkv_full, (1, 1))
    rest_low = rest_f32.astype(bf16)
    first_low = dot(tie(proj_low, rest_low)[:own_block], qkv_full, (1, 1))
    first_part = jnp.concatenate([first_low, rest_f32], axis=0)
    part_scale = latent_sum_all(first_part * normed_one)
    part_shift = latent_sum_all(first_part)
    grad_shifted_one = reduce_ctx(reduce_cores(first_low, rest_low))
    grad_stream = middle_grad + norm_back(
        normed_one[:share], inverse_one[:share], grad_shifted_one * (1.0 + mod_of(1, 1))
    )

    def token_out(v):
        v = to_global(v).reshape(latents, -1, width)
        n = v.shape[1]
        out = jnp.zeros((latents, own_rows, width), f32)
        for k in range(tens):
            piece = v if k == 0 else from_core(v, k)
            out = lax.dynamic_update_slice_in_dim(out, piece, ((tensor_at + k) % tens) * n, 1)
        return out

    grad_tokens = token_out(grad_stream)

    grad_mod = jnp.stack(
        [part_shift, part_scale, grad_gate_one, grad_shift_two, grad_scale_two, grad_gate_two], axis=1
    ).reshape(latents * 6, width)
    packet = jnp.concatenate([grad_mod, bias_output[None], bias_contract[None]], axis=0)
    packet = dot(packet, col_order_f32, (1, 1), precision=HIGHEST)
    total = packet[:, :cols_c]
    qkv_grad_low = grad_low(shifted_one, tie(proj_low, packet))
    output_grad_low = grad_low(attn_low, tie(attended, proj_low))
    both_low = jnp.concatenate([qkv_grad_low, output_grad_low], axis=1)
    owned_qkv = reduce_shards(both_low, qkv_high)()
    for k in range(1, tens):
        total = total + from_core(packet[:, k * cols_c : (k + 1) * cols_c], -k)
    side = jnp.concatenate([bias_qv.reshape(-1), bias_expand])
    flat = jnp.concatenate([total.reshape(-1), side])
    summed = total
    slot = lax.broadcasted_iota(jnp.int32, (ctxs, 1), 0)
    side_all = jnp.zeros((ctxs, side.size), f32)
    n_total = total.size
    for k in range(ctxs):
        got = flat if k == 0 else from_ctx(flat, k)
        if k:
            summed = summed + got[:n_total].reshape(total.shape)
        side_all = jnp.where(slot == (ctx_at + k) % ctxs, got[n_total:], side_all)
    qv_pad = side_all[:, : 2 * cols].reshape(ctxs, 2, cols).transpose(1, 0, 2).reshape(2, cols_c)
    expand_pad = side_all[:, 2 * cols :].reshape(hid_c)
    result = token_out(tie(result_share, summed))
    message = jnp.concatenate([summed.reshape(-1), qv_pad.reshape(-1), expand_pad])[None]
    gathered = gather_shards(message)()
    n_mod = latents * 6 * cols_c
    mod_all = gathered[:, :n_mod].reshape(shards * latents, 6 * cols_c)
    sums = jnp.sum(gathered[:, n_mod:], axis=0)
    out_cols, con_cols = sums[:cols_c], sums[cols_c : 2 * cols_c]
    grad_qv_bias = sums[2 * cols_c : 4 * cols_c].reshape(2, cols_c)
    grad_expand_bias = sums[4 * cols_c :]
    grad_ada_bias = jnp.sum(mod_all, axis=0).reshape(6, cols_c)
    own_cols = blk // ctxs
    squashed_own = lax.dynamic_slice_in_dim(squashed_all, (shard_at * ctxs + ctx_at) * own_cols, own_cols, 1)
    grad_ada = dot(squashed_own.astype(f32), mod_all, (0, 0), precision=HIGHEST).reshape(own_cols, 6, cols_c)
    cond_part = dot(mod_all, ada_flat.astype(f32), (1, 1), precision=HIGHEST)
    tail = jnp.concatenate([cond_part.reshape(-1), out_cols, con_cols])
    n_cond = cond_part.size
    cond_sum = cond_part
    vectors = jnp.zeros((2, width), f32)
    for k in range(tens):
        got = tail if k == 0 else from_core(tail, k)
        if k:
            cond_sum = cond_sum + got[:n_cond].reshape(cond_part.shape)
        vectors = lax.dynamic_update_slice_in_dim(
            vectors, got[n_cond:].reshape(2, cols_c), ((tensor_at + k) % tens) * cols_c, 1
        )
    half = cond_sum.shape[0] // 2
    both = jnp.stack([cond_sum[:half], swap(cond_sum[half:], 1)], axis=1)
    both = both.reshape(shards // 2, latents, 2, blk)
    grad_squashed = jnp.zeros((latents, width), f32)
    for p in range(shards // 2):
        got = both[p] if p == 0 else swap(both[p], mask_of(p))
        for j in range(2):
            at = (shard_at ^ mask_of(p) ^ j) * blk
            grad_squashed = lax.dynamic_update_slice_in_dim(grad_squashed, got[:, j], at, 1)
    grad_cond = silu_back(condition.astype(f32), grad_squashed)

    def to_owner(v, widths):
        rows = blk // ctxs
        outs = [jnp.zeros((rows, n * ctxs), f32) for n in widths]
        for k in range(ctxs):
            piece = lax.dynamic_slice_in_dim(v, ((ctx_at - k) % ctxs) * rows, rows, 0)
            if k:
                piece = from_ctx(piece.astype(bf16), k).astype(f32)
            at = 0
            for i, n in enumerate(widths):
                outs[i] = lax.dynamic_update_slice_in_dim(
                    outs[i], piece[:, at : at + n], ((ctx_at + k) % ctxs) * n, 1
                )
                at += n
        return outs

    owned_early = jnp.concatenate([owned_expand(gathered), owned_contract(summed)], axis=1)
    grad_expand, grad_contract = to_owner(owned_early, (hid, hid))
    *grad_qkv, grad_output = to_owner(owned_qkv, (cols,) * 4)
    grad_qkv = jnp.stack(grad_qkv, axis=1)
    grad_contract, grad_output = grad_contract.T, grad_output.T
    return (
        result,
        grad_tokens,
        grad_cond,
        grad_ada,
        grad_ada_bias,
        grad_qkv,
        grad_qv_bias,
        grad_output,
        vectors[0],
        grad_expand,
        grad_expand_bias,
        grad_contract,
        vectors[1],
    )


def solution(mesh):
    in_specs = (
        P("shard", "ctx", None),
        P("shard", None),
        P("shard", None, "tensor"),
        P(None, "tensor"),
        P("shard", None, "tensor"),
        P(None, "tensor"),
        P("tensor", "shard"),
        P(),
        P("shard", "tensor"),
        P("tensor"),
        P("tensor", "shard"),
        P(),
        P("shard", "ctx", None),
    )
    out_specs = (
        P("shard", "ctx", None),
        P("shard", "ctx", None),
        P("shard", None),
        P(("shard", "ctx"), None, "tensor"),
        P(None, "tensor"),
        P(("shard", "ctx"), None, "tensor"),
        P(None, "tensor"),
        P("tensor", ("shard", "ctx")),
        P(),
        P(("shard", "ctx"), "tensor"),
        P("tensor"),
        P("tensor", ("shard", "ctx")),
        P(),
    )
    return jax.shard_map(layer, mesh=mesh, in_specs=in_specs, out_specs=out_specs, check_vma=False)
```

```python
import jax
import jax.numpy as jnp
from jax import lax
from jax.experimental import pallas as pl
from jax.experimental.pallas import tpu as pltpu
from jax.sharding import PartitionSpec as P

SHARD, CTX, TENSOR = "shard", "ctx", "tensor"
HD = 64
EPS = 1e-06
f32 = jnp.float32
bf16 = jnp.bfloat16
HIGHEST = lax.Precision.HIGHEST


def layer_norm(values):
    center = values - jnp.mean(values, axis=-1, keepdims=True)
    inverse_std = lax.rsqrt(jnp.mean(center * center, axis=-1, keepdims=True) + EPS)
    return (center * inverse_std, inverse_std)


def norm_back(normed, inverse_std, upstream):
    return (
        upstream
        - jnp.mean(upstream, axis=-1, keepdims=True)
        - normed * jnp.mean(upstream * normed, axis=-1, keepdims=True)
    ) * inverse_std


def gelu_tanh(values):
    return jax.nn.gelu(values, approximate=True)


def gelu_back(before, upstream):
    return jax.vjp(gelu_tanh, before)[1](upstream)[0]


def silu_back(before, upstream):
    return jax.vjp(jax.nn.silu, before)[1](upstream)[0]


def dot(a, b, contract, out=f32, precision=None):
    return lax.dot_general(
        a, b, ((contract[:1], contract[1:]), ((), ())), preferred_element_type=f32, precision=precision
    ).astype(out)


def _nt(a, b):
    return lax.dot_general(a, b, (((1,), (1,)), ((), ())), preferred_element_type=f32)


def _nn(a, b):
    return lax.dot_general(a, b, (((1,), (0,)), ((), ())), preferred_element_type=f32)


def _loop(rows, chunk, step):
    if rows == chunk:
        step(slice(0, rows))
        return

    def one(c, carry):
        step(pl.ds(pl.multiple_of(c * chunk, chunk), chunk))
        return carry

    lax.fori_loop(0, rows // chunk, one, 0)


def project_kernel(chunk, count, *refs):
    tok_ref, shift_ref, scale_ref, bias_ref = refs[:4]
    pieces, (low_ref, shifted_ref, weight_ref) = refs[4 : 4 + count], refs[4 + count :]
    n = weight_ref.shape[0] // count
    for p, piece in enumerate(pieces):
        weight_ref[p * n : (p + 1) * n, :] = piece[...]
    gain = 1.0 + scale_ref[...]

    def step(at):
        normed, _ = layer_norm(tok_ref[at, :].astype(f32))
        shifted = (normed * gain + shift_ref[...]).astype(bf16)
        shifted_ref[at, :] = shifted
        low_ref[at, :] = (_nn(shifted, weight_ref[...]) + bias_ref[...]).astype(bf16)

    _loop(tok_ref.shape[0], chunk, step)


def assemble_kernel(*refs):
    out_ref = refs[-1]
    n, half = refs[0].shape[0] // 2, out_ref.shape[0] // 2
    for p, ref in enumerate(refs[:-1]):
        out_ref[p * n : (p + 1) * n, :] = ref[:n, :]
        out_ref[half + p * n : half + (p + 1) * n, :] = ref[n:, :]


def assemble(pairs):
    rows, columns = pairs[0].shape
    return pl.pallas_call(
        assemble_kernel,
        out_shape=pltpu.VMEM((rows * len(pairs), columns), bf16),
        cost_estimate=_CHEAP,
        name="assemble",
    )(*pairs)


def project(tok, shift, scale, bias, pieces):
    rows, width = tok.shape
    columns = pieces[0].shape[1]
    return pl.pallas_call(
        lambda *refs: project_kernel(_chunk(rows), len(pieces), *refs),
        out_shape=[
            jax.ShapeDtypeStruct((rows, columns), bf16),
            jax.ShapeDtypeStruct((rows, width), bf16),
            jax.ShapeDtypeStruct((width, columns), bf16),
        ],
        cost_estimate=_CHEAP,
        name="project",
    )(tok, shift, scale, bias, *pieces)


def attend_kernel(chunk, q_ref, k_ref, v_ref, out_ref, stat_ref):
    rows, lanes = out_ref.shape
    heads = [slice(h * HD, (h + 1) * HD) for h in range(lanes // HD)]
    values_t = v_ref[...].T

    def step(at):
        outs = []
        for h, lane in enumerate(heads):
            queries = q_ref[at, lane] * bf16(HD**-0.5)
            scores = _nt(k_ref[:, lane], queries)
            top = jnp.max(scores, axis=0, keepdims=True)
            logsum = top + jnp.log(jnp.sum(jnp.exp(scores - top), axis=0, keepdims=True))
            probs = jnp.exp(scores - logsum).astype(bf16)
            outs.append(_nn(values_t[lane, :], probs))
            stat_ref[h : h + 1, at] = logsum
        out_ref[at, :] = jnp.concatenate(outs, axis=0).T.astype(bf16)

    _loop(rows, chunk, step)


def attend_back_kernel(
    chunk,
    steps,
    q_ref,
    k_ref,
    v_ref,
    grad_ref,
    out_ref,
    stat_ref,
    proj_ref,
    bias_ref,
    keys_acc,
    values_acc,
):
    rows, lanes = out_ref.shape
    scale = HD**-0.5
    heads = [slice(h * HD, (h + 1) * HD) for h in range(lanes // HD)]

    def columns(part):
        if steps == 1:
            return slice(part * lanes, (part + 1) * lanes)
        return pl.ds(pl.multiple_of((part * steps + pl.program_id(0)) * lanes, lanes), lanes)

    keys_t = k_ref[...].T
    keys_acc[...] = jnp.zeros_like(keys_acc)
    values_acc[...] = jnp.zeros_like(values_acc)
    bias_ref[...] = jnp.zeros_like(bias_ref)

    def step(at):
        grad_queries, grad_keys, grad_values = [], [], []
        product = (grad_ref[at, :].astype(f32) * out_ref[at, :].astype(f32)).T
        for h, lane in enumerate(heads):
            queries, grad = q_ref[at, lane], grad_ref[at, lane]
            row_dot = jnp.sum(product[lane, :], axis=0, keepdims=True)
            probs = jnp.exp(_nt(k_ref[:, lane], queries * bf16(scale)) - stat_ref[h : h + 1, at])
            grad_scores = (probs * (_nt(v_ref[:, lane], grad) - row_dot)).astype(bf16)
            grad_values.append(_nn(probs.astype(bf16), grad))
            grad_keys.append(_nn(grad_scores, queries))
            grad_queries.append(_nn(keys_t[lane, :], grad_scores))
        values_acc[...] += jnp.concatenate(grad_values, axis=1)
        keys_acc[...] += jnp.concatenate(grad_keys, axis=1)
        got = jnp.concatenate(grad_queries, axis=0).T * scale
        bias_ref[0:1, :] += jnp.sum(got, axis=0, keepdims=True)
        proj_ref[at, columns(0)] = got.astype(bf16)

    _loop(rows, chunk, step)
    proj_ref[:, columns(1)] = (keys_acc[...] * scale).astype(bf16)
    proj_ref[:, columns(2)] = values_acc[...].astype(bf16)
    bias_ref[1:2, :] = jnp.sum(values_acc[...], axis=0, keepdims=True)


def _chunk(rows):
    return 256 if rows % 256 == 0 else rows


_CHEAP = pl.CostEstimate(flops=1000, bytes_accessed=1000, transcendentals=0)


def _parts(qkv, lanes, steps):
    if steps == 1:
        arrays = [qkv[:, j * lanes : (j + 1) * lanes] for j in range(3)]
        return arrays, [pl.BlockSpec((qkv.shape[0], lanes), lambda i: (0, 0))] * 3
    specs = [
        pl.BlockSpec((qkv.shape[0], lanes), lambda i, j=j: (0, j * steps + i)) for j in range(3)
    ]
    return [qkv] * 3, specs


def attend(qkv, lanes):
    rows, steps = qkv.shape[0], qkv.shape[1] // (3 * lanes)
    parts, specs = _parts(qkv, lanes, steps)
    return pl.pallas_call(
        lambda *refs: attend_kernel(_chunk(rows), *refs),
        grid=(steps,),
        in_specs=specs,
        out_specs=[
            pl.BlockSpec((rows, lanes), lambda i: (0, i)),
            pl.BlockSpec((8, rows), lambda i: (i, 0)),
        ],
        out_shape=[
            jax.ShapeDtypeStruct((rows, steps * lanes), bf16),
            jax.ShapeDtypeStruct((8 * steps, rows), f32),
        ],
        cost_estimate=_CHEAP,
        name="attend",
    )(*parts)


def attend_back(qkv, grad, out, stat, lanes):
    rows, steps = qkv.shape[0], qkv.shape[1] // (3 * lanes)
    parts, specs = _parts(qkv, lanes, steps)
    own = pl.BlockSpec((rows, lanes), lambda i: (0, i))
    return pl.pallas_call(
        lambda *refs: attend_back_kernel(_chunk(rows), steps, *refs),
        grid=(steps,),
        in_specs=[
            *specs, own, own, pl.BlockSpec((8, rows), lambda i: (i, 0))
        ],
        out_specs=[
            pl.BlockSpec((rows, 3 * steps * lanes), lambda i: (0, 0)),
            pl.BlockSpec((8, lanes), lambda i: (i, 0)),
        ],
        out_shape=[
            jax.ShapeDtypeStruct((rows, 3 * steps * lanes), bf16),
            jax.ShapeDtypeStruct((8 * steps, lanes), f32),
        ],
        cost_estimate=_CHEAP,
        scratch_shapes=[pltpu.VMEM((rows, lanes), f32)] * 2,
        name="attend_back",
    )(*parts, grad, out, stat)


def layer(
    tokens,
    condition,
    ada_weight,
    ada_bias,
    qkv_weight,
    qv_bias,
    output_weight,
    output_bias,
    expand_weight,
    expand_bias,
    contract_weight,
    contract_bias,
    cotangent,
):
    latents, own_rows, width = tokens.shape
    shards = lax.axis_size(SHARD)
    ctxs = lax.axis_size(CTX)
    tens = lax.axis_size(TENSOR)
    shard_at = lax.axis_index(SHARD)
    ctx_at = lax.axis_index(CTX)
    tensor_at = lax.axis_index(TENSOR)
    blk = width // shards
    share = own_rows // tens
    cols_c = qkv_weight.shape[2]
    cols = cols_c // ctxs
    hid_c = expand_weight.shape[1]
    hid = hid_c // ctxs

    bits = shards.bit_length() - 1
    assert shards == 1 << bits

    def mask_of(place):
        return sum(((place >> i) & 1) << (bits - 1 - i) for i in range(bits))

    def swap(v, mask):
        return lax.ppermute(v, SHARD, [(s, s ^ mask) for s in range(shards)])

    def tie(v, *after):
        return lax.optimization_barrier((v, *after))[0]

    def from_ctx(v, k):
        return lax.ppermute(v, CTX, [(i, (i - k) % ctxs) for i in range(ctxs)])

    def from_core(v, k):
        return lax.ppermute(v, TENSOR, [(i, (i - k) % tens) for i in range(tens)])

    def gather_half(piece):
        parts = [piece]
        for p in range(1, shards // 2):
            parts.append(swap(piece, mask_of(p)))
        return parts

    def gather_direct(piece):
        n = shards // 2
        parts = [piece] * shards
        parts[n] = swap(piece, 1)
        for p in sorted(range(1, n), key=mask_of):
            parts[p] = swap(piece, mask_of(p))
            parts[n + p] = swap(parts[p], 1)
        return parts

    def gather_shards(piece, *after):
        parts = gather_half(piece)
        if after:
            parts = lax.optimization_barrier((*parts, *after))[: len(parts)]
        half = lax.optimization_barrier(jnp.concatenate(parts, axis=0))
        other = swap(half, 1)
        return lambda *late: jnp.concatenate([half, tie(other, *late) if late else other], axis=0)

    def pair_of(piece):
        return jnp.concatenate([piece, swap(piece, 1)], axis=0)

    def gather_pairs(pair, *late):
        got = [swap(pair, mask_of(p)) for p in range(1, shards // 2)]
        got = lax.optimization_barrier((*got, *late))[: len(got)]
        return assemble([pair, *got])

    def reduce_shards(low, high, *after):
        kind = high.dtype
        got = swap(high, 1)
        if after:
            got = tie(got, *after)
        n = low.shape[0] // (shards // 2)
        own = low[:n] + got[:n].astype(f32)
        sent = [
            (low[p * n : (p + 1) * n] + got[p * n : (p + 1) * n].astype(f32)).astype(kind)
            for p in range(1, shards // 2)
        ]
        pieces = []
        for p, piece in zip(range(1, shards // 2), sent):
            pieces.append(swap(piece, mask_of(p)))

        def total(*late):
            parts = lax.optimization_barrier((*pieces, *late))[: len(pieces)] if late else pieces
            return sum((v.astype(f32) for v in parts), own)

        return total

    def gather_group(v, *late):
        rows = [from_ctx(v, k) for k in range(1, ctxs)]
        rows = [v] + [tie(r, *late) if late else r for r in rows]
        rows = jnp.concatenate(rows, axis=0)
        others = [from_core(rows, k) for k in range(1, tens)]
        return jnp.concatenate([rows] + others, axis=0)

    def reduce_cores(first, rest):
        rows = ctxs * share
        total = first
        for k in range(1, tens):
            got = from_core(rest[(k - 1) * rows : k * rows], -k)
            total = total + got.astype(f32)
        return total

    def reduce_ctx(total, *late):
        own = total[:share]
        for k in range(1, ctxs):
            piece = total[k * share : (k + 1) * share].astype(bf16)
            got = from_ctx(piece, -k)
            own = own + (tie(got, *late) if late else got).astype(f32)
        return own

    rel = lax.broadcasted_iota(jnp.int32, (width, width), 1)
    row = lax.broadcasted_iota(jnp.int32, (width, width), 0)
    rel_blk = rel // blk
    rel_mask = sum(((rel_blk >> i) & 1) << (bits - 1 - i) for i in range(bits))
    rel_glob = (shard_at ^ rel_mask) * blk + rel % blk
    order = row == rel_glob
    row_glob = ((tensor_at + row // cols_c) % tens) * cols_c + row % cols_c
    col_order = row_glob == rel_glob
    order_low = order.astype(bf16)
    order_f32 = order.astype(f32)
    col_order_f32 = col_order.astype(f32)

    def to_global(v):
        a = v.astype(bf16)
        left = v - a.astype(f32)
        b = left.astype(bf16)
        c = (left - b.astype(f32)).astype(bf16)
        return dot(a, order_low, (1, 1)) + dot(b, order_low, (1, 1)) + dot(c, order_low, (1, 1))

    cond_all = gather_shards(condition)()
    squashed_all = jax.nn.silu(cond_all.astype(f32)).astype(bf16)
    squashed_rows = lax.dynamic_slice_in_dim(squashed_all, shard_at * blk, blk, 1)
    ada_flat = ada_weight.reshape(blk, 6 * cols_c)
    mod_part = dot(squashed_rows, ada_flat, (1, 0))
    half = mod_part.shape[0] // 2
    mod_sum = reduce_shards(mod_part[:half], mod_part[half:])()
    own_mod = mod_sum.reshape(latents * 6, cols_c)
    own_mod = own_mod + jnp.tile(ada_bias, (latents, 1))
    mod_cols = jnp.concatenate([own_mod] + [from_core(own_mod, k) for k in range(1, tens)], axis=1)
    modulation = dot(mod_cols, col_order_f32, (1, 0), precision=HIGHEST).reshape(latents, 6, width)

    def per_row(v, count):
        return v[:, None, :] if count is None else jnp.broadcast_to(v[:, None, :], (latents, count, width))

    def latent_rows(v, blocks):
        if latents == 1:
            return v
        return jnp.tile(jnp.repeat(v, share, axis=0), (blocks, 1))

    blocks = ctxs * tens
    rows_own = latents * share
    del per_row

    def ctx_cols(v, size, axis):
        return lax.dynamic_slice_in_dim(v, ctx_at * size, size, axis)

    lanes = min(cols, 2 * HD)
    steps = cols // lanes

    qkv_piece = ctx_cols(qkv_weight, cols, 2).reshape(blk, 3 * cols)
    out_piece = ctx_cols(output_weight, cols, 0).T
    expand_piece = ctx_cols(expand_weight, hid, 1)
    contract_piece = ctx_cols(contract_weight, hid, 0).T
    qkv_parts = gather_direct(qkv_piece)
    biases = dot(jnp.stack([output_bias, contract_bias]), order_f32, (1, 0), precision=HIGHEST)
    out_bias, con_bias = biases[0:1], biases[1:2]
    qv_own = ctx_cols(qv_bias, cols, 1)
    expand_own = ctx_cols(expand_bias, hid, 0)

    def own_rows_of(v):
        mine = lax.dynamic_slice_in_dim(v, tensor_at * share, share, 1).reshape(rows_own, width)
        return dot(mine, order_low, (1, 0), bf16)

    tok = gather_group(own_rows_of(tokens), mod_sum)
    cot_own = own_rows_of(cotangent)
    share = rows_own

    def mod_of(i, count):
        return latent_rows(modulation[:, i], count)

    stream = tok[:share].astype(f32)
    qkv_bias = jnp.concatenate([qv_own[0], jnp.zeros((cols,), f32), qv_own[1]])[None]
    contract_pair = pair_of(contract_piece)
    qkv_low, shifted_one, qkv_full = project(
        tok, modulation[:, 0], modulation[:, 1], qkv_bias, qkv_parts
    )
    cot = gather_group(cot_own, qkv_low)
    out_t = gather_shards(out_piece, qkv_low)()
    attended, stat = attend(qkv_low, lanes)
    expand_full = gather_shards(expand_piece, attended)()
    own_block = ctxs * share

    def core_product(a, b, contract):
        rest = dot(a[own_block:], b, contract, bf16)
        first = dot(a[:own_block], b, contract)
        return reduce_cores(first, rest)

    attn_core = core_product(attended, out_t, (1, 1))
    attn_share = reduce_ctx(attn_core) + out_bias
    gate_one, gate_two = mod_of(2, 1), mod_of(5, 1)
    middle_share = stream + gate_one * attn_share
    normed_two, inverse_two = layer_norm(middle_share)
    shifted_two = gather_group((normed_two * (1.0 + mod_of(4, 1)) + mod_of(3, 1)).astype(bf16))
    hidden_pre = dot(shifted_two, expand_full, (1, 0)) + expand_own
    hidden_act = gelu_tanh(hidden_pre).astype(bf16)
    contract_t = gather_pairs(contract_pair, hidden_act)

    def latent_sum(v):
        return jnp.sum(v.reshape(latents, -1, width), axis=1)

    def latent_sum_all(v):
        return jnp.sum(v.reshape(blocks, latents, -1, width), axis=(0, 2))

    def grad_high(a, g):
        return dot(a[:, width // 2 :], g, (0, 0), bf16)

    def grad_low(a, g):
        return dot(a[:, : width // 2], g, (0, 0))

    upstream_share = cot[:share].astype(f32)
    mlp_low = (cot.astype(f32) * mod_of(5, blocks)).astype(bf16)
    contract_high = grad_high(mlp_low, hidden_act)
    grad_act = dot(tie(mlp_low, contract_high), contract_t, (1, 0))
    grad_pre = gelu_back(hidden_pre, grad_act)
    bias_expand = jnp.sum(grad_pre, axis=0)
    pre_low = grad_pre.astype(bf16)
    two_core = core_product(pre_low, expand_full, (1, 1))
    grad_shifted_two = reduce_ctx(two_core)
    normed_one, inverse_one = layer_norm(tie(tok, two_core).astype(f32))
    bias_contract = jnp.sum(upstream_share * gate_two, axis=0)
    grad_scale_two = latent_sum(grad_shifted_two * normed_two)
    grad_shift_two = latent_sum(grad_shifted_two)
    middle_grad = upstream_share + norm_back(
        normed_two, inverse_two, grad_shifted_two * (1.0 + mod_of(4, 1))
    )
    grad_gate_one = latent_sum(middle_grad * attn_share)
    grad_attn = middle_grad * gate_one
    bias_output = jnp.sum(grad_attn, axis=0)
    low_share = grad_attn.astype(bf16)
    attn_low = gather_group(low_share)
    grad_attended = dot(attn_low, out_t, (1, 0), bf16)
    proj_low, bias_heads = attend_back(qkv_low, grad_attended, attended, stat, lanes)
    bias_heads = bias_heads.reshape(steps, 8, lanes)
    bias_qv = jnp.stack([bias_heads[:, 0].reshape(cols), bias_heads[:, 1].reshape(cols)])
    pre_late = tie(pre_low, two_core)
    expand_high = grad_high(shifted_two, pre_late)
    output_high = grad_high(attn_low, attended)
    mlp_core = core_product(tie(hidden_act, two_core), contract_t, (1, 1))
    owned_contract = reduce_shards(
        grad_low(mlp_low, tie(hidden_act, two_core)), contract_high, low_share
    )
    owned_expand = reduce_shards(grad_low(shifted_two, pre_late), expand_high, proj_low)
    mlp_share = reduce_ctx(mlp_core, proj_low) + con_bias
    result_share = middle_share + gate_two * mlp_share
    grad_gate_two = latent_sum(upstream_share * mlp_share)
    qkv_high = jnp.concatenate([grad_high(shifted_one, proj_low), output_high], axis=1)
    proj_late = tie(proj_low, qkv_high)
    rest_f32 = dot(proj_late[own_block:], qkv_full, (1, 1))
    rest_low = rest_f32.astype(bf16)
    first_low = dot(tie(proj_low, rest_low)[:own_block], qkv_full, (1, 1))
    first_part = jnp.concatenate([first_low, rest_f32], axis=0)
    part_scale = latent_sum_all(first_part * normed_one)
    part_shift = latent_sum_all(first_part)
    grad_shifted_one = reduce_ctx(reduce_cores(first_low, rest_low))
    grad_stream = middle_grad + norm_back(
        normed_one[:share], inverse_one[:share], grad_shifted_one * (1.0 + mod_of(1, 1))
    )

    def token_out(v):
        v = to_global(v).reshape(latents, -1, width)
        n = v.shape[1]
        out = jnp.zeros((latents, own_rows, width), f32)
        for k in range(tens):
            piece = v if k == 0 else from_core(v, k)
            out = lax.dynamic_update_slice_in_dim(out, piece, ((tensor_at + k) % tens) * n, 1)
        return out

    grad_tokens = token_out(grad_stream)

    grad_mod = jnp.stack(
        [part_shift, part_scale, grad_gate_one, grad_shift_two, grad_scale_two, grad_gate_two], axis=1
    ).reshape(latents * 6, width)
    packet = jnp.concatenate([grad_mod, bias_output[None], bias_contract[None]], axis=0)
    packet = dot(packet, col_order_f32, (1, 1), precision=HIGHEST)
    total = packet[:, :cols_c]
    qkv_grad_low = grad_low(shifted_one, tie(proj_low, packet))
    output_grad_low = grad_low(attn_low, tie(attended, proj_low))
    both_low = jnp.concatenate([qkv_grad_low, output_grad_low], axis=1)
    owned_qkv = reduce_shards(both_low, qkv_high)()
    for k in range(1, tens):
        total = total + from_core(packet[:, k * cols_c : (k + 1) * cols_c], -k)
    side = jnp.concatenate([bias_qv.reshape(-1), bias_expand])
    flat = jnp.concatenate([total.reshape(-1), side])
    summed = total
    slot = lax.broadcasted_iota(jnp.int32, (ctxs, 1), 0)
    side_all = jnp.zeros((ctxs, side.size), f32)
    n_total = total.size
    for k in range(ctxs):
        got = flat if k == 0 else from_ctx(flat, k)
        if k:
            summed = summed + got[:n_total].reshape(total.shape)
        side_all = jnp.where(slot == (ctx_at + k) % ctxs, got[n_total:], side_all)
    qv_pad = side_all[:, : 2 * cols].reshape(ctxs, 2, cols).transpose(1, 0, 2).reshape(2, cols_c)
    expand_pad = side_all[:, 2 * cols :].reshape(hid_c)
    result = token_out(tie(result_share, summed))
    message = jnp.concatenate([summed.reshape(-1), qv_pad.reshape(-1), expand_pad])[None]
    gathered = gather_shards(message)()
    n_mod = latents * 6 * cols_c
    mod_all = gathered[:, :n_mod].reshape(shards * latents, 6 * cols_c)
    sums = jnp.sum(gathered[:, n_mod:], axis=0)
    out_cols, con_cols = sums[:cols_c], sums[cols_c : 2 * cols_c]
    grad_qv_bias = sums[2 * cols_c : 4 * cols_c].reshape(2, cols_c)
    grad_expand_bias = sums[4 * cols_c :]
    grad_ada_bias = jnp.sum(mod_all, axis=0).reshape(6, cols_c)
    own_cols = blk // ctxs
    squashed_own = lax.dynamic_slice_in_dim(squashed_all, (shard_at * ctxs + ctx_at) * own_cols, own_cols, 1)
    grad_ada = dot(squashed_own.astype(f32), mod_all, (0, 0), precision=HIGHEST).reshape(own_cols, 6, cols_c)
    cond_part = dot(mod_all, ada_flat.astype(f32), (1, 1), precision=HIGHEST)
    tail = jnp.concatenate([cond_part.reshape(-1), out_cols, con_cols])
    n_cond = cond_part.size
    cond_sum = cond_part
    vectors = jnp.zeros((2, width), f32)
    for k in range(tens):
        got = tail if k == 0 else from_core(tail, k)
        if k:
            cond_sum = cond_sum + got[:n_cond].reshape(cond_part.shape)
        vectors = lax.dynamic_update_slice_in_dim(
            vectors, got[n_cond:].reshape(2, cols_c), ((tensor_at + k) % tens) * cols_c, 1
        )
    half = cond_sum.shape[0] // 2
    both = jnp.stack([cond_sum[:half], swap(cond_sum[half:], 1)], axis=1)
    both = both.reshape(shards // 2, latents, 2, blk)
    grad_squashed = jnp.zeros((latents, width), f32)
    for p in range(shards // 2):
        got = both[p] if p == 0 else swap(both[p], mask_of(p))
        for j in range(2):
            at = (shard_at ^ mask_of(p) ^ j) * blk
            grad_squashed = lax.dynamic_update_slice_in_dim(grad_squashed, got[:, j], at, 1)
    grad_cond = silu_back(condition.astype(f32), grad_squashed)

    def to_owner(v, widths):
        rows = blk // ctxs
        outs = [jnp.zeros((rows, n * ctxs), f32) for n in widths]
        for k in range(ctxs):
            piece = lax.dynamic_slice_in_dim(v, ((ctx_at - k) % ctxs) * rows, rows, 0)
            if k:
                piece = from_ctx(piece.astype(bf16), k).astype(f32)
            at = 0
            for i, n in enumerate(widths):
                outs[i] = lax.dynamic_update_slice_in_dim(
                    outs[i], piece[:, at : at + n], ((ctx_at + k) % ctxs) * n, 1
                )
                at += n
        return outs

    owned_early = jnp.concatenate([owned_expand(gathered), owned_contract(summed)], axis=1)
    grad_expand, grad_contract = to_owner(owned_early, (hid, hid))
    *grad_qkv, grad_output = to_owner(owned_qkv, (cols,) * 4)
    grad_qkv = jnp.stack(grad_qkv, axis=1)
    grad_contract, grad_output = grad_contract.T, grad_output.T
    return (
        result,
        grad_tokens,
        grad_cond,
        grad_ada,
        grad_ada_bias,
        grad_qkv,
        grad_qv_bias,
        grad_output,
        vectors[0],
        grad_expand,
        grad_expand_bias,
        grad_contract,
        vectors[1],
    )


def solution(mesh):
    in_specs = (
        P(SHARD, CTX, None),
        P(SHARD, None),
        P(SHARD, None, TENSOR),
        P(None, TENSOR),
        P(SHARD, None, TENSOR),
        P(None, TENSOR),
        P(TENSOR, SHARD),
        P(),
        P(SHARD, TENSOR),
        P(TENSOR),
        P(TENSOR, SHARD),
        P(),
        P(SHARD, CTX, None),
    )
    out_specs = (
        P(SHARD, CTX, None),
        P(SHARD, CTX, None),
        P(SHARD, None),
        P((SHARD, CTX), None, TENSOR),
        P(None, TENSOR),
        P((SHARD, CTX), None, TENSOR),
        P(None, TENSOR),
        P(TENSOR, (SHARD, CTX)),
        P(),
        P((SHARD, CTX), TENSOR),
        P(TENSOR),
        P(TENSOR, (SHARD, CTX)),
        P(),
    )
    return jax.shard_map(layer, mesh=mesh, in_specs=in_specs, out_specs=out_specs, check_vma=False)
```
